32 devices in a mesh: ctx: 4 (over y, x), head: 8 (over z, core).
Axes of the slice: x: 2, y: 2, z: 4, core: 2. Of those that a mesh axis runs over, the one named last changes fastest.
Arguments:
- hidden_rows: float32 [512, 2304], P(('ctx', 'head')), may hold values from -60 to 60
- segment_ids: int32 [512], replicated, may hold values from 0 to 1, never falling along the last dimension, each value on 1 to 480 neighbouring positions
- w_query: float32 [2304, 6144], P(None, 'head'), may hold values from -0.125 to 0.125
- w_down: float32 [2304, 576], replicated, may hold values from -0.125 to 0.125
- w_up: float32 [512, 8192], P(None, 'head'), may hold values from -0.25 to 0.25
- w_out: float32 [4096, 2304], P('head'), may hold values from -0.09375 to 0.09375
Outputs:
- attended: float32 [512, 2304], P(('ctx', 'head'))
- log_norm: float32 [32, 512], P('head', 'ctx')
The draws below stay inside these ranges and needn't reach their ends.
All inputs are finite; a program needn't handle non-finite values.
Results may differ from the reference program's by a relative error of at most 0.00015.
Values sent between devices are 32-bit elements; how exact they have to be, the bound alone decides.
No kernel may reach another device: no remote copies, remote signals or barrier semaphores. Data moves between devices by JAX's collectives and lax.ppermute only.
A program may use at most 64 MiB of HBM per device.

```python
import math
import jax
import jax.numpy as jnp
import numpy as np
from jax import lax

D = 2304
H = 32
KV_RANK = 512
NOPE = 128
ROPE = 64
VDIM = 128
TOK_CTX = 128
TOKENS = 512


def draw_hidden_rows(key, part):
    first, second = jax.random.split(key, 2)
    row_scales = jnp.exp(jax.random.uniform(first, (TOKENS, 1), minval=-0.3, maxval=0.3))
    values = jnp.clip(jax.random.normal(second, (TOKENS, D)), -6.0, 6.0) * row_scales
    return jnp.clip(values, -60.0, 60.0).astype(jnp.float32)


def levels(rng, extent, cuts, least, high):
    def one(dim, blocks):
        heights = jax.random.uniform(jax.random.fold_in(jax.random.fold_in(rng, 6), dim), (blocks,), jnp.float32, least / len(cuts), high / len(cuts))
        return jnp.repeat(jnp.exp(heights), extent[dim] // blocks).reshape((-1,) + (1,) * (len(extent) - dim - 1))

    level = one(*cuts[0])
    for cut in cuts[1:]:
        level = level * one(*cut)
    return level


def length_profile(amount, total, reach, lean):
    weights = [(1 << 20) // math.isqrt(rank ** lean) + 1 for rank in range(2, amount + 1)]
    spare, counts = total - reach - (amount - 1), [1] * (amount - 1)
    while spare > 0:
        free = [i for i in range(amount - 1) if counts[i] < reach]
        whole, left = sum([weights[i] for i in free]), spare
        for i in free:
            addition = min(reach - counts[i], max(1, left * weights[i] // whole), spare)
            counts[i] = counts[i] + addition
            spare = spare - addition
    return np.array([reach] + counts)


def uneven_parts(rng, amount, total, most, lean):
    if amount == 2:
        one = jax.random.randint(rng, (), max(1, total - most), min(most, total - 1) + 1)
        return jnp.stack([one, total - one])
    tallies = jnp.asarray(length_profile(amount, total, most, lean), jnp.int32)
    pairs = (amount - 1) // 2
    giver, receiver = tallies[1:1 + 2 * pairs:2], tallies[2:2 + 2 * pairs:2]
    slack = jnp.minimum(giver - 1, most - receiver)
    passed = jax.random.randint(jax.random.fold_in(rng, 1), (pairs,), 0, 1 << 20) % (slack + 1)
    tallies = tallies.at[1:1 + 2 * pairs:2].set(giver - passed).at[2:2 + 2 * pairs:2].set(receiver + passed)
    return tallies[jax.random.permutation(jax.random.fold_in(rng, 2), amount)]


def scatter_about(stream_key, dims, spread, most, pieces=(), held_as=jnp.bfloat16):
    array = spread * jax.random.normal(stream_key, dims, jnp.float32)
    if pieces:
        array = array * levels(stream_key, dims, pieces, -0.22, 0.18)
    return jnp.clip(array, -most, most).astype(held_as)


def setup_inputs(seed: int = 0) -> dict:
    seeds = jax.random.split(jax.random.key(seed), 7)
    hidden_rows = draw_hidden_rows(jax.random.fold_in(seeds[6], 71), 0)
    segment_ids = jnp.searchsorted(jnp.cumsum(uneven_parts(seeds[1], 2, TOKENS, TOKENS - TOK_CTX // 4, 0)), jnp.arange(TOKENS), side="right").astype(jnp.int32)
    w_query = scatter_about(seeds[2], (D, H * (NOPE + ROPE)), D ** -0.5, 0.125, ((1, 8),), jnp.float32)
    w_down = scatter_about(seeds[3], (D, KV_RANK + ROPE), D ** -0.5, 0.125, (), jnp.float32)
    w_up = scatter_about(seeds[4], (KV_RANK, H * (NOPE + VDIM)), KV_RANK ** -0.5, 0.25, ((1, 8),), jnp.float32)
    w_out = scatter_about(seeds[5], (H * VDIM, D), (H * VDIM) ** -0.5, 0.09375, ((0, 8),), jnp.float32)
    return {"hidden_rows": hidden_rows, "segment_ids": segment_ids, "w_query": w_query, "w_down": w_down, "w_up": w_up, "w_out": w_out}


eps_norm = 1e-06
neg_fill = -1e+30
precise = lax.Precision.HIGHEST

def product(left, right):
    return jnp.dot(left, right, precision=precise, preferred_element_type=jnp.float32)

def normalize(raw_latent):
    compressed = raw_latent[:, :KV_RANK]
    mean_square = lax.optimization_barrier(jnp.mean(compressed * compressed, axis=1, keepdims=True))
    return jnp.concatenate([compressed * lax.rsqrt(mean_square + eps_norm), raw_latent[:, KV_RANK:]], axis=1)

def reference(hidden_rows, segment_ids, w_query, w_down, w_up, w_out):
    queries = product(hidden_rows, w_query).reshape(TOKENS, H, NOPE + ROPE).transpose(1, 0, 2)
    latent = normalize(product(hidden_rows, w_down))
    up_proj = product(latent[:, :KV_RANK], w_up).reshape(TOKENS, H, NOPE + VDIM).transpose(1, 0, 2)
    shared = latent[:, KV_RANK:]
    positions = jnp.arange(TOKENS, dtype=jnp.int32)
    allowed = (positions[None, :] <= positions[:, None]) & (segment_ids[None, :] == segment_ids[:, None])
    score_factor = 1.0 / math.sqrt(NOPE + ROPE)

    def per_head(operands):
        head_query, head_up = operands
        keys = jnp.concatenate([head_up[:, :NOPE], shared], axis=1)
        scores = jnp.dot(head_query, keys.T, precision=precise, preferred_element_type=jnp.float32) * score_factor
        scores = jnp.where(allowed, scores, neg_fill)
        peak = lax.optimization_barrier(jnp.max(scores, axis=1))
        weights = jnp.where(allowed, jnp.exp(scores - peak[:, None]), 0.0)
        total = lax.optimization_barrier(jnp.sum(weights, axis=1))
        result = product(weights, head_up[:, NOPE:]) / total[:, None]
        return (result, peak + jnp.log(total))
    outputs, log_norm = lax.map(per_head, (queries, up_proj))
    flattened = outputs.transpose(1, 0, 2).reshape(TOKENS, H * VDIM)
    return (product(flattened, w_out), log_norm)
```

```python
import math

import jax
import jax.numpy as jnp
from jax import lax
from jax.sharding import PartitionSpec as P

KV_RANK = 512
NOPE = 128
ROPE = 64
VDIM = 128

eps_norm = 1e-06
neg_fill = -1e30
precise = lax.Precision.HIGH


def product(left, right):
    return jnp.dot(left, right, precision=precise, preferred_element_type=jnp.float32)


def partner_swap(value):
    count = lax.axis_size("head")
    return lax.ppermute(value, "head", [(i, i ^ 1) for i in range(count)])


def chip_shift(value, step):
    count = lax.axis_size("head")
    return lax.ppermute(value, "head", [(i, (i + 2 * step) % count) for i in range(count)])


def gather_head(block):
    count = lax.axis_size("head")
    chips = count // 2
    me = lax.axis_index("head")
    chip, core = me // 2, me % 2
    mine = jnp.stack([block] + [chip_shift(block, s) for s in range(1, chips)])
    theirs = partner_swap(mine)
    first = jnp.where(core == 0, mine, theirs)
    second = jnp.where(core == 0, theirs, mine)
    both = jnp.concatenate([first, second], axis=1)
    order = (chip - jnp.arange(chips)) % chips
    both = jnp.take(both, order, axis=0)
    return both.reshape(-1, block.shape[1])


def scatter_head(partial):
    count = lax.axis_size("head")
    chips = count // 2
    rows = partial.shape[0] // count
    me = lax.axis_index("head")
    chip, core = me // 2, me % 2
    blocks = partial.reshape(chips, 2, rows, partial.shape[1])
    keep = lax.dynamic_index_in_dim(blocks, core, 1, keepdims=False)
    give = lax.dynamic_index_in_dim(blocks, 1 - core, 1, keepdims=False)
    pair = keep + partner_swap(give)
    total = lax.dynamic_index_in_dim(pair, chip, 0, keepdims=False)
    for s in range(1, chips):
        out = lax.dynamic_index_in_dim(pair, (chip + s) % chips, 0, keepdims=False)
        total = total + chip_shift(out, s)
    return total


def body(hidden_rows, segment_ids, w_query, w_down, w_up, w_out):
    ctx_count = lax.axis_size("ctx")
    ctx_at = lax.axis_index("ctx")
    head_count = w_query.shape[1] // (NOPE + ROPE)
    score_factor = 1.0 / math.sqrt(NOPE + ROPE)
    hidden = gather_head(hidden_rows)
    row_count = hidden.shape[0]
    raw = product(hidden, w_down)
    compressed = raw[:, :KV_RANK]
    mean_square = jnp.mean(compressed * compressed, axis=1, keepdims=True)
    latent = jnp.concatenate([compressed * lax.rsqrt(mean_square + eps_norm), raw[:, KV_RANK:]], axis=1)
    blocks = [latent]
    for step in range(1, ctx_count):
        pairs = [(i, i + step) for i in range(ctx_count - step)]
        blocks.append(lax.ppermute(latent, "ctx", pairs))
    queries = product(hidden, w_query).reshape(row_count, head_count, NOPE + ROPE)
    keys_all = jnp.concatenate(blocks, axis=0)
    offsets = jnp.arange(row_count, dtype=jnp.int32)
    key_pos = jnp.concatenate([(ctx_at - step) * row_count + offsets for step in range(ctx_count)])
    query_pos = ctx_at * row_count + offsets
    key_seg = jnp.take(segment_ids, jnp.maximum(key_pos, 0))
    query_seg = key_seg[:row_count]
    allowed = (
        (key_pos[None, :] <= query_pos[:, None])
        & (key_seg[None, :] == query_seg[:, None])
        & (key_pos >= 0)[None, :]
    )
    up = product(keys_all[:, :KV_RANK], w_up).reshape(-1, head_count, NOPE + VDIM)
    scores = jnp.einsum("qhd,khd->hqk", queries[..., :NOPE], up[..., :NOPE], precision=precise)
    scores = scores + jnp.einsum("qhd,kd->hqk", queries[..., NOPE:], keys_all[:, KV_RANK:], precision=precise)
    scores = jnp.where(allowed[None], scores * score_factor, neg_fill)
    peak = jnp.max(scores, axis=2)
    weights = jnp.where(allowed[None], jnp.exp(scores - peak[..., None]), 0.0)
    total = jnp.sum(weights, axis=2)
    out = jnp.einsum("hqk,khd->qhd", weights, up[..., NOPE:], precision=precise)
    out = out / total.T[..., None]
    log_norm = peak + jnp.log(total)
    partial = product(out.reshape(row_count, head_count * VDIM), w_out)
    return (scatter_head(partial), log_norm)


def solution(mesh):
    in_specs = (
        P(("ctx", "head"), None),
        P(),
        P(None, "head"),
        P(),
        P(None, "head"),
        P("head", None),
    )
    out_specs = (P(("ctx", "head"), None), P("head", "ctx"))
    return jax.shard_map(body, mesh=mesh, in_specs=in_specs, out_specs=out_specs, check_vma=False)
```

```python
import functools
import math

import jax
import jax.numpy as jnp
from jax import lax
from jax.experimental import pallas as pl
from jax.experimental.pallas import tpu as pltpu
from jax.sharding import PartitionSpec as P

KV_RANK = 512
NOPE = 128
ROPE = 64
VDIM = 128
QK = NOPE + ROPE

eps_norm = 1e-06
neg_fill = -1e30
F32 = jnp.float32
BF16 = jnp.bfloat16
VM = pl.BlockSpec(memory_space=pltpu.VMEM)
SM = pl.BlockSpec(memory_space=pltpu.SMEM)
NT = (((1,), (1,)), ((), ()))
NN = (((1,), (0,)), ((), ()))


def split(value):
    high = value.astype(BF16)
    return high, (value - high.astype(F32)).astype(BF16)


def dot3(left, right, dims=NN):
    rows = left[0].shape[0]
    stacked = lax.dot_general(
        jnp.concatenate(left, axis=0), right[0], dims, preferred_element_type=F32
    )
    rest = lax.dot_general(left[0], right[1], dims, preferred_element_type=F32)
    return stacked[:rows] + (stacked[rows:] + rest)


def latent_kernel(x_ref, w_ref, o_ref, acc):
    at = pl.program_id(0)

    @pl.when(at == 0)
    def _():
        acc[...] = jnp.zeros_like(acc)

    acc[...] += dot3(split(x_ref[...]), split(w_ref[...]), NT)

    @pl.when(at == pl.num_programs(0) - 1)
    def _():
        raw = acc[...]
        part = raw[:, :KV_RANK]
        mean_square = jnp.mean(part * part, axis=1, keepdims=True)
        o_ref[:, :KV_RANK] = part * lax.rsqrt(mean_square + eps_norm)
        o_ref[:, KV_RANK:] = raw[:, KV_RANK:]


def own_latent(x, w_down):
    rows, depth = x.shape
    wide = w_down.shape[1]
    step = depth // 3
    return pl.pallas_call(
        latent_kernel,
        grid=(3,),
        in_specs=[
            pl.BlockSpec((rows, step), lambda i: (0, i)),
            pl.BlockSpec((wide, step), lambda i: (0, i)),
        ],
        out_specs=pl.BlockSpec((rows, wide), lambda i: (0, 0)),
        out_shape=jax.ShapeDtypeStruct((rows, wide), F32),
        scratch_shapes=[pltpu.VMEM((rows, wide), F32)],
        compiler_params=pltpu.CompilerParams(vmem_limit_bytes=12 << 20),
        cost_estimate=pl.CostEstimate(
            flops=6 * rows * depth * wide, bytes_accessed=4 * depth * wide, transcendentals=0
        ),
        name="own_latent",
    )(x, w_down.T)


def keys_kernel(count, hc, *refs):
    lat = refs[:count]
    w_ref, kh_ref, kl_ref, vh_ref, vl_ref, wh, wl = refs[count:]
    wh[...], wl[...] = split(w_ref[...])
    weight = (wh[...], wl[...])
    at = 0
    for ref in lat:
        rows = ref.shape[0]
        up = dot3(split(ref[:, :KV_RANK]), weight)
        sh, sl = split(ref[:, KV_RANK:])
        for h in range(hc):
            base = h * (NOPE + VDIM)
            high, low = split(up[:, base : base + NOPE])
            kh_ref[h, at : at + rows, :NOPE] = high
            kl_ref[h, at : at + rows, :NOPE] = low
            kh_ref[h, at : at + rows, NOPE:] = sh
            kl_ref[h, at : at + rows, NOPE:] = sl
            high, low = split(up[:, base + NOPE : base + NOPE + VDIM])
            vh_ref[h, at : at + rows, :] = high
            vl_ref[h, at : at + rows, :] = low
        at += rows


def keys_values(latents, w_up):
    hc = w_up.shape[1] // (NOPE + VDIM)
    total = sum(a.shape[0] for a in latents)
    key = jax.ShapeDtypeStruct((hc, total, QK), BF16)
    val = jax.ShapeDtypeStruct((hc, total, VDIM), BF16)
    return pl.pallas_call(
        functools.partial(keys_kernel, len(latents), hc),
        in_specs=[VM] * (len(latents) + 1),
        out_specs=[VM] * 4,
        out_shape=[key, key, val, val],
        scratch_shapes=[pltpu.VMEM(w_up.shape, BF16)] * 2,
        compiler_params=pltpu.CompilerParams(vmem_limit_bytes=24 << 20),
        cost_estimate=pl.CostEstimate(
            flops=6 * total * KV_RANK * w_up.shape[1], bytes_accessed=4 << 20, transcendentals=0
        ),
        name="keys_values",
    )(*latents, w_up)


def attend_kernel(chips, ctx_count, hc, rows, *refs):
    blocks = refs[: 2 * chips]
    (w_ref, at_ref, kh_ref, kl_ref, vh_ref, vl_ref, o_ref, n_ref, xs, acc) = refs[2 * chips :]
    step = pl.program_id(0)
    chip, core, ctx, cut = at_ref[0], at_ref[1], at_ref[2], at_ref[3]
    size = rows * 2 * chips

    for n, ref in enumerate(blocks):
        other, s = n // chips, n % chips
        src = 2 * lax.rem(chip - s + chips, chips) + (core if other == 0 else 1 - core)
        high, low = split(ref[...])
        place = pl.multiple_of(src * rows, rows)
        xs[pl.ds(place, rows), :] = high
        xs[pl.ds(size + place, rows), :] = low
    wh, wl = split(w_ref[...])
    stacked = jnp.dot(xs[...], wh, preferred_element_type=F32)
    part = stacked[:size] + (stacked[size:] + jnp.dot(xs[:size], wl, preferred_element_type=F32))

    @pl.when(step == 0)
    def _():
        acc[...] = part

    @pl.when(step > 0)
    def _():
        acc[...] += part

    @pl.when(step == pl.num_programs(0) - 1)
    def _():
        total_keys = kh_ref.shape[1]
        half = rows * chips
        idx = lax.broadcasted_iota(jnp.int32, (1, total_keys), 1)
        which = idx // half
        shard_slot = lax.rem(which, ctx_count)
        flip = which // ctx_count
        inside = lax.rem(idx, half)
        src = lax.rem(chip - inside // rows + chips, chips)
        src = 2 * src + (core ^ flip)
        key_pos = (ctx ^ shard_slot) * size + src * rows + lax.rem(inside, rows)
        query_pos = ctx * size + lax.broadcasted_iota(jnp.int32, (size, 1), 0)
        allowed = (key_pos <= query_pos) & ((key_pos >= cut) | (query_pos < cut))
        factor = 1.0 / math.sqrt(QK)
        for h in range(hc):
            q = split(acc[:, h * QK : (h + 1) * QK])
            scores = dot3(q, (kh_ref[h], kl_ref[h]), NT) * factor
            scores = jnp.where(allowed, scores, neg_fill)
            peak = jnp.max(scores, axis=1, keepdims=True)
            weights = jnp.where(allowed, jnp.exp(scores - peak), 0.0)
            total = jnp.sum(weights, axis=1, keepdims=True)
            out = dot3(split(weights), (vh_ref[h], vl_ref[h]))
            o_ref[:, h * VDIM : (h + 1) * VDIM] = out / total
            n_ref[:, h : h + 1] = peak + jnp.log(total)


def attend(blocks, place, w_query, keys):
    hc = keys[0].shape[0]
    rows, depth = blocks[0].shape
    chips = len(blocks) // 2
    size = rows * len(blocks)
    total_keys = keys[0].shape[1]
    wide = w_query.shape[1]
    steps = 3
    part = depth // steps
    return pl.pallas_call(
        functools.partial(attend_kernel, chips, total_keys // size, hc, rows),
        grid=(steps,),
        in_specs=[pl.BlockSpec((rows, part), lambda i: (0, i))] * len(blocks)
        + [pl.BlockSpec((part, wide), lambda i: (i, 0)), SM]
        + [VM] * 4,
        out_specs=[
            pl.BlockSpec((size, hc * VDIM), lambda i: (0, 0)),
            pl.BlockSpec((size, hc), lambda i: (0, 0)),
        ],
        out_shape=[
            jax.ShapeDtypeStruct((size, hc * VDIM), F32),
            jax.ShapeDtypeStruct((size, hc), F32),
        ],
        scratch_shapes=[pltpu.VMEM((2 * size, part), BF16), pltpu.VMEM((size, wide), F32)],
        compiler_params=pltpu.CompilerParams(vmem_limit_bytes=40 << 20),
        cost_estimate=pl.CostEstimate(
            flops=6 * size * depth * wide, bytes_accessed=12 << 20, transcendentals=0
        ),
        name="attend",
    )(*blocks, w_query, place, *keys)


def project_kernel(chips, rows, x_ref, w_ref, at_ref, give_ref, keep_ref, acc):
    chip, core = at_ref[0], at_ref[1]
    acc[...] = dot3(split(x_ref[...]), split(w_ref[...]))
    for s in range(chips):
        dst = 2 * lax.rem(chip + s, chips)
        mine = pl.multiple_of((dst + core) * rows, rows)
        theirs = pl.multiple_of((dst + 1 - core) * rows, rows)
        keep_ref[s * rows : (s + 1) * rows, :] = acc[pl.ds(mine, rows), :]
        give_ref[s * rows : (s + 1) * rows, :] = acc[pl.ds(theirs, rows), :]


def project(x, place, w_out, chips):
    size, depth = x.shape
    wide = w_out.shape[1]
    rows = size // (2 * chips)
    steps = 3
    part = wide // steps
    half = jax.ShapeDtypeStruct((size // 2, wide), F32)
    return pl.pallas_call(
        functools.partial(project_kernel, chips, rows),
        grid=(steps,),
        in_specs=[
            pl.BlockSpec((size, depth), lambda i: (0, 0)),
            pl.BlockSpec((depth, part), lambda i: (0, i)),
            SM,
        ],
        out_specs=[pl.BlockSpec((size // 2, part), lambda i: (0, i))] * 2,
        out_shape=[half, half],
        scratch_shapes=[pltpu.VMEM((size, part), F32)],
        compiler_params=pltpu.CompilerParams(vmem_limit_bytes=24 << 20),
        cost_estimate=pl.CostEstimate(
            flops=6 * size * depth * wide, bytes_accessed=8 << 20, transcendentals=0
        ),
        name="project",
    )(x, w_out, place)


def partner_swap(value):
    count = lax.axis_size("head")
    return lax.ppermute(value, "head", [(i, i ^ 1) for i in range(count)])


def chip_shift(value, step):
    count = lax.axis_size("head")
    return lax.ppermute(value, "head", [(i, (i + 2 * step) % count) for i in range(count)])


def shard_send(value, flip):
    count = lax.axis_size("ctx")
    pairs = [(i, i ^ flip) for i in range(count) if i < i ^ flip < count]
    return lax.ppermute(value, "ctx", pairs)


def body(hidden_rows, segment_ids, w_query, w_down, w_up, w_out):
    ctx_count = lax.axis_size("ctx")
    chips = lax.axis_size("head") // 2
    ctx_at = lax.axis_index("ctx")
    me = lax.axis_index("head")
    cut = jnp.sum((segment_ids == 0).astype(jnp.int32))
    place = jnp.stack([me // 2, me % 2, ctx_at, cut]).astype(jnp.int32)
    rows = hidden_rows.shape[0]

    mine = [hidden_rows] + [chip_shift(hidden_rows, s) for s in range(1, chips)]
    latent = own_latent(hidden_rows, w_down)
    column = jnp.concatenate([latent] + [chip_shift(latent, s) for s in range(1, chips)])
    lat = [column] + [shard_send(column, f) for f in range(1, ctx_count)]
    keys = keys_values(lat + [partner_swap(a) for a in lat], w_up)
    blocks = mine + [partner_swap(a) for a in mine]
    out, norm = attend(blocks, place, w_query, keys)
    give, keep = project(out, place, w_out, chips)
    pair = keep + partner_swap(give)
    total = pair[:rows]
    for s in range(1, chips):
        total = total + chip_shift(pair[s * rows : (s + 1) * rows], s)
    return (total, norm.T)


def solution(mesh):
    in_specs = (
        P(("ctx", "head"), None),
        P(),
        P(None, "head"),
        P(),
        P(None, "head"),
        P("head", None),
    )
    out_specs = (P(("ctx", "head"), None), P("head", "ctx"))
    return jax.shard_map(body, mesh=mesh, in_specs=in_specs, out_specs=out_specs, check_vma=False)
```
